32 devices in a mesh: node: 8 (over y, x, core), local: 4 (over z).
Axes of the slice: x: 2, y: 2, z: 4, core: 2. Of those that a mesh axis runs over, the one named last changes fastest.
Arguments:
- tokens: bfloat16 [16384, 6144], P(('node', 'local')), may hold values from -6 to 6
- cotangent: bfloat16 [16384, 6144], P(('node', 'local')), may hold values from -0.5 to 0.5
- gate_weight: bfloat16 [6144, 512], P('local'), may hold values from -0.078125 to 0.078125
- up_weight: bfloat16 [6144, 512], P('local'), may hold values from -0.078125 to 0.078125
- down_weight: bfloat16 [512, 6144], P(None, 'local'), may hold values from -0.25 to 0.25
- alive: int32 [8], replicated, may hold values from 0 to 1, as said below
Outputs:
- grad_gate: float32 [6144, 512], P(('node', 'local'))
- grad_up: float32 [6144, 512], P(('node', 'local'))
- grad_down: float32 [512, 6144], P(None, ('node', 'local'))
The draws below stay inside these ranges and needn't reach their ends.
Inputs may be any that keep to these rules, and one draw needn't show every extreme that they name: `alive`: exactly one node is absent.
All inputs are finite; a program needn't handle non-finite values.
Results may differ from the reference program's by a relative error of at most 0.014.
Values may be sent and summed in bfloat16 or wider, within the bound.
A program may use at most 128 MiB of HBM per device.

```python
import jax
import jax.numpy as jnp
from jax import lax

D = 6144
FF = 512
TOK_DEV = 512
NODES = 8
TOKENS = 16384
N_LOCAL = 4


def draw_alive(key, part):
    order = jax.random.permutation(key, NODES)
    return (order[0] != jnp.arange(NODES)).astype(jnp.int32)


def spiked(entries, rng, source, target, parts, factor):
    def block_of(position):
        return (jnp.arange(entries.shape[position]) // (entries.shape[position] // parts)).reshape((-1,) + (1,) * (entries.ndim - 1 - position))

    first = jax.random.permutation(rng, parts)[block_of(target)]
    second = (block_of(target) + parts // 2) % parts
    return jnp.where((block_of(source) == first) | (block_of(source) == second), factor * entries, entries)


def level_of(stream_key, shape, split, least, high):
    factor_of = 1.0
    for dim, blocks in split:
        draws = jax.random.uniform(jax.random.fold_in(jax.random.fold_in(stream_key, 6), dim), (blocks,), jnp.float32, least / len(split), high / len(split))
        factor_of = factor_of * jnp.repeat(jnp.exp(draws), shape[dim] // blocks).reshape((-1,) + (1,) * (len(shape) - 1 - dim))
    return factor_of


def scatter_about(rng, shape, scale, reach, shards=(), dtype=jnp.bfloat16):
    entries = jax.random.normal(rng, shape, jnp.float32) * scale
    if len(shards) > 0:
        entries = level_of(rng, shape, shards, -0.22, 0.18) * entries
    return jnp.clip(entries, min=-reach, max=reach).astype(dtype)


def gaussian_with(key, extent, scale, limit, cuts, heavy, held_as=jnp.bfloat16):
    result = scale * jax.random.normal(key, extent, jnp.float32)
    if cuts:
        result = result * level_of(key, extent, cuts, -0.22, 0.18)
    return jnp.clip(spiked(result, jax.random.fold_in(key, 3), *heavy), -limit, limit).astype(held_as)


def setup_inputs(seed: int = 0) -> dict:
    arg_keys = jax.random.split(jax.random.key(seed), 7)
    tokens = gaussian_with(arg_keys[0], (TOKENS, D), 1.0, 6.0, ((0, 32),), (0, 1, 32, 2.75))
    cotangent = gaussian_with(arg_keys[1], (TOKENS, D), 0.0625, 0.5, ((0, 32),), (0, 1, 32, 2.75))
    gate_weight = scatter_about(arg_keys[2], (D, FF), D ** -0.5, 0.078125, ((0, 4),))
    up_weight = scatter_about(arg_keys[3], (D, FF), D ** -0.5, 0.078125, ((0, 4),))
    down_weight = scatter_about(arg_keys[4], (FF, D), FF ** -0.5, 0.25, ((1, 4),))
    alive = draw_alive(jax.random.fold_in(arg_keys[6], 71), 0)
    return dict(tokens=tokens, cotangent=cotangent, gate_weight=gate_weight, up_weight=up_weight, down_weight=down_weight, alive=alive)


def reference(tokens, cotangent, gate_weight, up_weight, down_weight, alive):
    blocks = tokens.shape[0] // TOK_DEV
    width = tokens.shape[1]
    hidden_units = gate_weight.shape[1]
    token_blocks = tokens.reshape(blocks, TOK_DEV, width)
    cot_blocks = cotangent.reshape(blocks, TOK_DEV, width)
    node_of = (jnp.arange(blocks) // N_LOCAL).astype(jnp.int32)
    keep_blocks = alive[node_of]

    def accumulate(carry, inputs):
        block_x, block_c, keep_one = inputs
        gate = jnp.dot(block_x, gate_weight, preferred_element_type=jnp.float32)
        up = jnp.dot(block_x, up_weight, preferred_element_type=jnp.float32)
        sig = jax.nn.sigmoid(gate)
        act = gate * sig
        hidden = (act * up).astype(jnp.bfloat16)
        masked = jnp.where(keep_one > 0, block_c, jnp.zeros_like(block_c))
        d_hidden = jnp.dot(masked, down_weight.T, preferred_element_type=jnp.float32)
        d_gate = (d_hidden * up * sig * (1.0 + gate * (1.0 - sig))).astype(jnp.bfloat16)
        d_up = (d_hidden * act).astype(jnp.bfloat16)
        part_gate = jnp.dot(block_x.T, d_gate, preferred_element_type=jnp.float32).astype(jnp.bfloat16)
        part_up = jnp.dot(block_x.T, d_up, preferred_element_type=jnp.float32).astype(jnp.bfloat16)
        part_down = jnp.dot(hidden.T, masked, preferred_element_type=jnp.float32).astype(jnp.bfloat16)
        return (carry[0] + part_gate.astype(jnp.float32), carry[1] + part_up.astype(jnp.float32), carry[2] + part_down.astype(jnp.float32)), None

    start = (jnp.zeros((width, hidden_units), jnp.float32), jnp.zeros((width, hidden_units), jnp.float32), jnp.zeros((hidden_units, width), jnp.float32))
    sums, _ = lax.scan(accumulate, start, (token_blocks, cot_blocks, keep_blocks))
    scale = 1.0 / jnp.sum(alive).astype(jnp.float32)
    return sums[0] * scale, sums[1] * scale, sums[2] * scale
```

```python
import functools

import jax
import jax.numpy as jnp
from jax import lax
from jax.experimental import pallas as pl
from jax.experimental.pallas import tpu as pltpu
from jax.sharding import PartitionSpec as P

MESH = pl.DeviceIdType.MESH
VMEM_LIMIT = 60 * 2**20
AHEAD = 2
CUTS = 2


class Place:
    def __init__(self, n_node, n_local):
        self.n_x = n_node // 4
        self.n_local = n_local
        self.pairs = n_node // 2
        self.node = lax.axis_index("node")
        self.z = lax.axis_index("local")
        self.core = lax.rem(self.node, 2)
        self.x = lax.rem(self.node // 2, self.n_x)
        self.y = self.node // (2 * self.n_x)

    def x_off(self, k):
        return lax.rem(self.x + k + self.n_x, self.n_x)

    def z_off(self, k):
        return lax.rem(self.z + k + self.n_local, self.n_local)

    def sibling(self):
        return (self.node + 1 - 2 * self.core, self.z)

    def x_peer(self, k):
        return ((self.y * self.n_x + self.x_off(k)) * 2 + self.core, self.z)

    def y_peer(self):
        return (((1 - self.y) * self.n_x + self.x) * 2 + self.core, self.z)

    def z_peer(self, k):
        return (self.node, self.z_off(k))

    def barrier(self):
        peers = [self.sibling(), self.y_peer()]
        peers += [self.x_peer(k) for k in range(1, self.n_x)]
        peers += [self.z_peer(k) for k in range(1, self.n_local)]
        sem = pltpu.get_barrier_semaphore()
        for peer in peers:
            pl.semaphore_signal(sem, inc=1, device_id=peer, device_id_type=MESH)
        pl.semaphore_wait(sem, len(peers))


def ffn_kernel(
    n_node, n_local, tok_in, cot_in, keep, w_gate, w_up, w_down, out,
    full_gate, full_up, full_down, acc, tok, cot, v_gate, v_up, v_down, grads,
    away, from_core, held, rx1, ry1, rx2, ry2, rz,
    load_sem, g_send, g_recv, core_send, core_recv, r_send, r_recv,
):
    at = Place(n_node, n_local)
    n_x, pairs = at.n_x, at.pairs
    depth, units = w_gate.shape
    wide = units // CUTS
    own = (w_gate, w_up, w_down)
    full = (full_gate, full_up, full_down)
    step = (depth // n_node, depth // n_node, wide // n_node)
    half = (wide // 2, wide // 2, depth // 2)
    n_tok = tok.shape[0]
    tile = 256 if n_tok % 256 == 0 else n_tok
    rows = tok.shape[1] // n_node
    part = rows // n_local
    f32 = jnp.float32
    started = []

    def remote(send_sem, recv_sem, i, slot, src, dst, peer):
        return pltpu.make_async_remote_copy(
            src_ref=src, dst_ref=dst, send_sem=send_sem.at[i, slot], recv_sem=recv_sem.at[i, slot],
            device_id=peer, device_id_type=MESH,
        )

    def send_with(send_sem, recv_sem):
        def send(i, slot, src, dst, peer):
            op = remote(send_sem, recv_sem, i, slot, src, dst, peer)
            op.start()
            started.append(op)

        def arrived(i, slot, ref, peer):
            remote(send_sem, recv_sem, i, slot, ref, ref, peer).wait_recv()

        return send, arrived

    send_g, arrived_g = send_with(g_send, g_recv)
    items = [(c, w, k) for c in range(CUTS) for w in range(3) for k in range(1, n_local)]
    AZ, BY, CORE = 0, 1, 2
    BX, CY, CX = 3, 3 + (n_x - 1), 3 + 2 * (n_x - 1)

    def piece(core, y, x):
        return core * pairs + y * n_x + x

    def span(w, first, count, base=0):
        return pl.ds(pl.multiple_of(base + first * step[w], step[w]), count * step[w])

    mine = piece(at.core, at.y, at.x)

    def stage_a(i):
        c, w, k = items[i]
        if w == 2:
            src = w_down.at[span(w, mine, 1, c * wide)]
        else:
            src = own[w].at[span(w, mine, 1), pl.ds(c * wide, wide)]
        send_g(i, AZ, src, full[w].at[c, k - 1, span(w, mine, 1)], at.z_peer(k))

    def stage_b(i):
        c, w, k = items[i]
        block = full[w].at[c, k - 1, span(w, mine, 1)]
        arrived_g(i, AZ, block, at.z_peer(k))
        for j in range(1, n_x):
            send_g(i, BX + j - 1, block, block, at.x_peer(j))
        send_g(i, BY, block, block, at.y_peer())

    def stage_c(i):
        c, w, k = items[i]
        for j in range(1, n_x):
            r = span(w, piece(at.core, at.y, at.x_off(-j)), 1)
            arrived_g(i, BX + j - 1, full[w].at[c, k - 1, r], at.x_peer(j))
            block = full[w].at[c, k - 1, r, pl.ds(0, half[w])]
            send_g(i, CY + j - 1, block, block, at.y_peer())
        r = span(w, piece(at.core, 1 - at.y, at.x), 1)
        arrived_g(i, BY, full[w].at[c, k - 1, r], at.y_peer())
        block = full[w].at[c, k - 1, r, pl.ds(half[w], half[w])]
        for j in range(1, n_x):
            send_g(i, CX + j - 1, block, block, at.x_peer(j))

    def stage_d(i):
        c, w, k = items[i]
        for j in range(1, n_x):
            r = span(w, piece(at.core, 1 - at.y, at.x_off(-j)), 1)
            arrived_g(i, CY + j - 1, full[w].at[c, k - 1, r, pl.ds(0, half[w])], at.y_peer())
            arrived_g(i, CX + j - 1, full[w].at[c, k - 1, r, pl.ds(half[w], half[w])], at.x_peer(j))
        block = full[w].at[c, k - 1, span(w, at.core * pairs, pairs)]
        send_g(i, CORE, block, block, at.sibling())

    def multiply(w, shard, weight, first):
        left = cot if w == 2 else tok
        columns = pl.ds(pl.multiple_of(shard * depth, 128), depth)
        dims = (((1,), (1,)), ((), ())) if w == 2 else (((1,), (0,)), ((), ()))

        def body(r, _):
            at_rows = pl.ds(pl.multiple_of(r * tile, tile), tile)
            term = lax.dot_general(left[at_rows, columns], weight[...], dims, preferred_element_type=f32)
            acc[w, at_rows, :] = term if first else acc[w, at_rows, :] + term
            return 0

        lax.fori_loop(0, n_tok // tile, body, 0)

    def stage_e(i):
        c, w, k = items[i]
        arrived_g(i, CORE, full[w].at[c, k - 1, span(w, (1 - at.core) * pairs, pairs)], at.sibling())
        multiply(w, at.z_off(-k), full[w].at[c, k - 1], False)

    def own_terms(c, w):
        cut = pl.ds(c * wide, wide)
        weight = v_down.at[cut] if w == 2 else (v_gate, v_up)[w].at[:, cut]
        multiply(w, at.z, weight, True)

    def gather_step(s):
        if s + AHEAD < len(items):
            stage_a(s + AHEAD)
        for lag, stage in enumerate((stage_b, stage_c, stage_d, stage_e)):
            if 0 <= s - lag < len(items):
                stage(s - lag)

    band = 64 if n_tok % 64 == 0 else n_tok

    def pointwise(c):
        def body(r, _):
            at_rows = pl.ds(pl.multiple_of(r * band, band), band)
            gate, up = acc[0, at_rows, :], acc[1, at_rows, :]
            alive = jnp.full(gate.shape, keep[at.node], jnp.int32) > 0
            d_hidden = jnp.where(alive, acc[2, at_rows, :], 0.0)
            sig = jax.nn.sigmoid(gate)
            act = gate * sig
            grads[c, 0, at_rows, :] = (d_hidden * up * sig * (1.0 + gate * (1.0 - sig))).astype(grads.dtype)
            grads[c, 1, at_rows, :] = (d_hidden * act).astype(grads.dtype)
            grads[c, 2, at_rows, :] = jnp.where(alive, act * up, 0.0).astype(grads.dtype)
            return 0

        lax.fori_loop(0, n_tok // band, body, 0)

    send_r, arrived_r = send_with(r_send, r_recv)
    n_items = 3 * CUTS
    X1, Y1 = 0, 2 * (n_x - 1)
    Y2 = Y1 + n_x
    X2 = Y2 + 1
    Z = X2 + n_x - 1
    lo, hi = pl.ds(0, wide // 2), pl.ds(wide // 2, wide // 2)

    def product(i, p, core):
        c, t = divmod(i, 3)
        columns = pl.ds(pl.multiple_of((p * 2 + core) * rows, 128), rows)
        left = cot if t == 2 else tok
        return lax.dot_general(
            left[:, columns], grads[c, t], (((0,), (0,)), ((), ())), preferred_element_type=f32
        )

    def core_copy(i, p):
        return remote(core_send, core_recv, i, p, away.at[i % 2, p], from_core.at[i % 2, p], at.sibling())

    def other(i):
        def body(p, _):
            term = product(i, p, 1 - at.core).astype(away.dtype)
            if i >= 2:
                core_copy(i - 2, p).wait_send()
            away[i % 2, p] = term
            core_copy(i, p).start()
            return 0

        lax.fori_loop(0, pairs, body, 0)

    def same(i):
        def body(p, _):
            term = product(i, p, at.core)
            core_copy(i, p).wait_recv()
            held[i, p] = (term + from_core[i % 2, p].astype(f32)).astype(held.dtype)
            return 0

        lax.fori_loop(0, pairs, body, 0)

    def block(y, x):
        return y * n_x + x

    def first(i):
        for far in range(2):
            y = at.y if far else 1 - at.y
            for k in range(1, n_x):
                send_r(i, X1 + 2 * (k - 1) + far, held.at[i, block(y, at.x_off(k)), :, lo], rx1.at[i, k - 1, far], at.x_peer(k))
            for k in range(n_x - 1, n_x) if far else range(n_x - 1):
                x = at.x_off(k + 1)
                send_r(i, Y1 + k, held.at[i, block(1 - at.y, x), :, hi], ry1.at[i, k], at.y_peer())

    def second(i):
        p = block(1 - at.y, at.x)
        total = held[i, p, :, lo].astype(f32)
        for k in range(1, n_x):
            arrived_r(i, X1 + 2 * (k - 1), rx1.at[i, k - 1, 0], at.x_peer(k))
            total = total + rx1[i, k - 1, 0].astype(f32)
        held[i, p, :, lo] = total.astype(held.dtype)
        send_r(i, Y2, held.at[i, p, :, lo], ry2.at[i], at.y_peer())
        for k in range(1, n_x):
            p = block(at.y, at.x_off(k))
            arrived_r(i, Y1 + k - 1, ry1.at[i, k - 1], at.y_peer())
            held[i, p, :, hi] = (held[i, p, :, hi].astype(f32) + ry1[i, k - 1].astype(f32)).astype(held.dtype)
            send_r(i, X2 + k - 1, held.at[i, p, :, hi], rx2.at[i, k - 1], at.x_peer(k))

    def third(i):
        p = block(at.y, at.x)
        total = held[i, p, :, lo].astype(f32)
        for k in range(1, n_x):
            arrived_r(i, X1 + 2 * (k - 1) + 1, rx1.at[i, k - 1, 1], at.x_peer(k))
            total = total + rx1[i, k - 1, 1].astype(f32)
        arrived_r(i, Y2, ry2.at[i], at.y_peer())
        held[i, p, :, lo] = (total + ry2[i].astype(f32)).astype(held.dtype)
        arrived_r(i, Y1 + n_x - 1, ry1.at[i, n_x - 1], at.y_peer())
        total = held[i, p, :, hi].astype(f32) + ry1[i, n_x - 1].astype(f32)
        for k in range(1, n_x):
            arrived_r(i, X2 + k - 1, rx2.at[i, k - 1], at.x_peer(k))
            total = total + rx2[i, k - 1].astype(f32)
        held[i, p, :, hi] = total.astype(held.dtype)
        for k in range(1, n_local):
            slot = pl.ds(pl.multiple_of(at.z_off(k) * part, part), part)
            send_r(i, Z + k - 1, held.at[i, p, slot], rz.at[i, k - 1], at.z_peer(k))

    def fourth(i):
        c, t = divmod(i, 3)
        slot = pl.ds(pl.multiple_of(at.z * part, part), part)
        total = held[i, block(at.y, at.x), slot, :].astype(f32)
        for k in range(1, n_local):
            arrived_r(i, Z + k - 1, rz.at[i, k - 1], at.z_peer(k))
            total = total + rz[i, k - 1].astype(f32)
        out[t, :, pl.ds(c * wide, wide)] = total

    loads = [
        pltpu.make_async_copy(src, dst, load_sem.at[n])
        for n, (src, dst) in enumerate(
            ((tok_in, tok), (w_gate, v_gate), (w_up, v_up), (cot_in, cot), (w_down, v_down))
        )
    ]
    for load in loads:
        load.start()
    at.barrier()
    for i in range(AHEAD):
        stage_a(i)
    for w, needs in enumerate((loads[:2], loads[2:3], loads[3:])):
        for load in needs:
            load.wait()
        own_terms(0, w)

    todo = []
    per = len(items) // CUTS
    for s in range(len(items) + 3):
        gather_step(s)
        if s >= 3 and (s - 3) % per == per - 1:
            c = (s - 3) // per
            for stage, i in todo:
                stage(i)
            pointwise(c)
            todo = []
            for i in range(3 * c, 3 * c + 3):
                todo += [(other, i), (same, i), (first, i)]
                for lag, stage in enumerate((second, third, fourth)):
                    if 0 <= i - 1 - lag:
                        todo.append((stage, i - 1 - lag))
            if c + 1 < CUTS:
                for w in range(3):
                    own_terms(c + 1, w)
        elif todo:
            stage, i = todo.pop(0)
            stage(i)
            if todo and todo[0][0] is first:
                stage, i = todo.pop(0)
                stage(i)
    for stage, i in todo:
        stage(i)
    for s in range(n_items, n_items + 3):
        for lag, stage in enumerate((second, third, fourth)):
            if s - 1 - lag < n_items:
                stage(s - 1 - lag)
    for op in started:
        op.wait_send()

    def drain(p, _):
        for i in range(n_items - 2, n_items):
            core_copy(i, p).wait_send()
        return 0

    lax.fori_loop(0, pairs, drain, 0)


def on_device(tokens, cotangent, gate_weight, up_weight, down_weight, alive):
    n_node = lax.axis_size("node")
    n_local = lax.axis_size("local")
    n_x = n_node // 4
    n_tok, width = tokens.shape
    depth, units = gate_weight.shape
    bf16 = tokens.dtype
    vmem = pl.BlockSpec(memory_space=pltpu.VMEM)
    hbm = pl.BlockSpec(memory_space=pl.ANY)
    wide = units // CUTS
    half = wide // 2
    rows = width // n_node
    pairs = n_node // 2
    part = rows // n_local
    g_items = 3 * CUTS * (n_local - 1)
    g_slots = 3 + 3 * (n_x - 1)
    r_items = 3 * CUTS
    r_slots = 2 * (n_x - 1) + n_x + 1 + (n_x - 1) + (n_local - 1)
    sums = pl.pallas_call(
        functools.partial(ffn_kernel, n_node, n_local),
        out_shape=jax.ShapeDtypeStruct((3, part, units), jnp.float32),
        in_specs=[hbm, hbm, pl.BlockSpec(memory_space=pltpu.SMEM), hbm, hbm, hbm],
        out_specs=vmem,
        scratch_shapes=[
            pltpu.VMEM((CUTS, n_local - 1, depth, wide), bf16),
            pltpu.VMEM((CUTS, n_local - 1, depth, wide), bf16),
            pltpu.VMEM((CUTS, n_local - 1, wide, depth), bf16),
            pltpu.VMEM((3, n_tok, wide), jnp.float32),
            pltpu.VMEM((n_tok, width), bf16),
            pltpu.VMEM((n_tok, width), bf16),
            pltpu.VMEM((depth, units), bf16),
            pltpu.VMEM((depth, units), bf16),
            pltpu.VMEM((units, depth), bf16),
            pltpu.VMEM((CUTS, 3, n_tok, wide), bf16),
            pltpu.VMEM((2, pairs, rows, wide), bf16),
            pltpu.VMEM((2, pairs, rows, wide), bf16),
            pltpu.VMEM((r_items, pairs, rows, wide), bf16),
            pltpu.VMEM((r_items, n_x - 1, 2, rows, half), bf16),
            pltpu.VMEM((r_items, n_x, rows, half), bf16),
            pltpu.VMEM((r_items, n_x - 1, rows, half), bf16),
            pltpu.VMEM((r_items, rows, half), bf16),
            pltpu.VMEM((r_items, n_local - 1, part, wide), bf16),
            pltpu.SemaphoreType.DMA((5,)),
            pltpu.SemaphoreType.DMA((g_items, g_slots)),
            pltpu.SemaphoreType.DMA((g_items, g_slots)),
            pltpu.SemaphoreType.DMA((r_items, pairs)),
            pltpu.SemaphoreType.DMA((r_items, pairs)),
            pltpu.SemaphoreType.DMA((r_items, r_slots)),
            pltpu.SemaphoreType.DMA((r_items, r_slots)),
        ],
        compiler_params=pltpu.CompilerParams(
            collective_id=0, has_side_effects=True, vmem_limit_bytes=VMEM_LIMIT
        ),
        name="ffn_backward",
    )(tokens, cotangent, alive, gate_weight, up_weight, down_weight)
    scale = 1.0 / jnp.sum(alive).astype(jnp.float32)
    return (sums[0] * scale, sums[1] * scale, (sums[2] * scale).T)


def solution(mesh):
    in_specs = (
        P(("node", "local"), None),
        P(("node", "local"), None),
        P("local", None),
        P("local", None),
        P(None, "local"),
        P(),
    )
    out_specs = (P(("node", "local"), None), P(("node", "local"), None), P(None, ("node", "local")))
    return jax.shard_map(
        on_device, mesh=mesh, in_specs=in_specs, out_specs=out_specs, check_vma=False
    )
```
